32 devices in a mesh: depth: 16 (over z, x, core), lat: 2 (over y).
Axes of the slice: x: 2, y: 2, z: 4, core: 2. Of those that a mesh axis runs over, the one named last changes fastest.
Arguments:
- waves_in: float32 [16, 4, 4, 16, 1024], P('depth', None, None, 'lat'), may hold values from -6 to 6
- surface_waves: float32 [4, 4, 16, 1024], P(None, None, 'lat'), may hold values from -6 to 6
- slowness: float32 [16, 4, 16, 1024], P('depth', None, 'lat'), may hold values from 0.22 to 0.67
- section_planes: int32 [16], P('depth'), may hold values from 1 to 4, 48 in all
- block_freqs: int32 [16, 4], P('depth'), may hold values from 0 to 63
- surface_freqs: int32 [4], replicated, may hold values from 0 to 63
Outputs:
- waves_out: float32 [16, 4, 4, 16, 1024], P('depth', None, None, 'lat')
- image: float32 [16, 4, 16, 1024], P('depth', None, 'lat')
The draws below stay inside these ranges and needn't reach their ends.
Inputs may be any that keep to these rules, and one draw needn't show every extreme that they name: `section_planes`: some section has exactly 4 active planes; the counts sum to 48.
All inputs are finite; a program needn't handle non-finite values. No bound on the sum of `section_planes` on one device may be relied on, other than what follows from the above.
Results may differ from the reference program's by a relative error of at most 0.0003.
Values sent between devices are 32-bit elements; how exact they have to be, the bound alone decides.
A program may use at most 64 MiB of HBM per device.

```python
import math
import jax
import jax.numpy as jnp
import numpy as np
from jax import lax

NY = 1024
FB = 4
PLANES = 4
NF = 64
SECTIONS = 16
NX = 16


def set_ends(array, key, low, top_value):
    index_at = [jax.random.randint(jax.random.fold_in(key, axis), (), 0, length) for axis, length in enumerate(array.shape)]
    longest = array.shape.index(max(array.shape))
    neighbour = index_at[:longest] + [(index_at[longest] + 1) % array.shape[longest]] + index_at[longest + 1:]
    return array.at[tuple(index_at)].set(low).at[tuple(neighbour)].set(top_value)


def levels(own_key, extent, pieces, low, largest):
    gain = 1.0
    for axis_at, shards_of in pieces:
        heights = jax.random.uniform(jax.random.fold_in(jax.random.fold_in(own_key, 6), axis_at), (shards_of,), jnp.float32, low / len(pieces), largest / len(pieces))
        gain = gain * jnp.repeat(jnp.exp(heights), extent[axis_at] // shards_of).reshape((-1,) + (1,) * (len(extent) - 1 - axis_at))
    return gain


def split_up(count, total, reach, slope):
    portions = [(1 << 20) // math.isqrt(grade ** slope) + 1 for grade in range(2, count + 1)]
    rest, counts = total - reach - (count - 1), [1] * (count - 1)
    while rest > 0:
        movable = [i for i in range(count - 1) if counts[i] < reach]
        whole, budget = sum([portions[i] for i in movable]), rest
        for i in movable:
            extra = min(reach - counts[i], max(1, budget * portions[i] // whole), rest)
            counts[i] = counts[i] + extra
            rest = rest - extra
    return np.array([reach] + counts)


def uneven_parts(rng, number_of, total, reach, slope):
    if number_of == 2:
        one = jax.random.randint(rng, (), max(1, total - reach), min(reach, total - 1) + 1)
        return jnp.stack([one, total - one])
    tallies = jnp.asarray(split_up(number_of, total, reach, slope), jnp.int32)
    twos = (number_of - 1) // 2
    giver, sink = tallies[1:1 + 2 * twos:2], tallies[2:2 + 2 * twos:2]
    margin = jnp.minimum(giver - 1, reach - sink)
    shifted = jax.random.randint(jax.random.fold_in(rng, 1), (twos,), 0, 1 << 20) % (margin + 1)
    tallies = tallies.at[1:1 + 2 * twos:2].set(giver - shifted).at[2:2 + 2 * twos:2].set(sink + shifted)
    return tallies[jax.random.permutation(jax.random.fold_in(rng, 2), number_of)]


def scatter_about(own_key, dims, spread, limit, cuts=(), dtype=jnp.bfloat16):
    drawn = jax.random.normal(own_key, dims, jnp.float32) * spread
    if len(cuts) > 0:
        drawn = levels(own_key, dims, cuts, -0.22, 0.18) * drawn
    return jnp.clip(drawn, min=-limit, max=limit).astype(dtype)


def setup_inputs(seed: int = 0) -> dict:
    key_of = jax.random.split(jax.random.key(seed), 7)
    return {
        "waves_in": scatter_about(key_of[0], (SECTIONS, FB, 4, NX, NY), 1.0, 6.0, ((0, 16), (3, 2)), jnp.float32),
        "surface_waves": scatter_about(key_of[1], (FB, 4, NX, NY), 1.0, 6.0, ((2, 2),), jnp.float32),
        "slowness": jnp.clip(jnp.exp(math.log(0.67) - 1.1136502 * jax.random.uniform(key_of[2], (SECTIONS, PLANES, NX, NY), jnp.float32) ** levels(key_of[2], (SECTIONS, PLANES, NX, NY), ((0, 16), (2, 2)), -0.2, 0.2)), 0.22, 0.67),
        "section_planes": uneven_parts(key_of[3], SECTIONS, SECTIONS * PLANES * 3 // 4, PLANES, 1).astype(jnp.int32),
        "block_freqs": set_ends(jax.random.randint(key_of[4], (SECTIONS, FB), 0, NF), jax.random.fold_in(key_of[4], 1), 0, NF - 1).astype(jnp.int32),
        "surface_freqs": set_ends(jax.random.randint(key_of[5], (FB,), 0, NF), jax.random.fold_in(key_of[5], 1), 0, NF - 1).astype(jnp.int32),
    }


DEPTH_STEP = 0.02
SMOOTHING = 0.4
BASE_HERTZ = 8.0
HERTZ_STEP = 0.5
DIFFRACTION_TOP = 0.2


def angular_of(freqs):
    return 2.0 * math.pi * (BASE_HERTZ + HERTZ_STEP * freqs.astype(jnp.float32))


def diffraction_of(pulsation):
    return DIFFRACTION_TOP * (2.0 * math.pi * BASE_HERTZ) / pulsation


def phase_shifted(fields, slowness_slab, pulsation):
    phase = pulsation[:, None, None] * slowness_slab[None] * DEPTH_STEP
    cosine_part = jnp.cos(phase)
    sine_part = jnp.sin(phase)
    source_real = fields[:, 0] * cosine_part - fields[:, 1] * sine_part
    source_imag = fields[:, 0] * sine_part + fields[:, 1] * cosine_part
    receiver_real = fields[:, 2] * cosine_part + fields[:, 3] * sine_part
    receiver_imag = fields[:, 3] * cosine_part - fields[:, 2] * sine_part
    return jnp.stack([source_real, source_imag, receiver_real, receiver_imag], 1)


def filtered(fields, second_diff, diffraction):
    source_real = fields[:, 0] + SMOOTHING * second_diff[:, 0] - diffraction * second_diff[:, 1]
    source_imag = fields[:, 1] + SMOOTHING * second_diff[:, 1] + diffraction * second_diff[:, 0]
    receiver_real = fields[:, 2] + SMOOTHING * second_diff[:, 2] + diffraction * second_diff[:, 3]
    receiver_imag = fields[:, 3] + SMOOTHING * second_diff[:, 3] - diffraction * second_diff[:, 2]
    return jnp.stack([source_real, source_imag, receiver_real, receiver_imag], 1)


def across_columns(fields, diffraction):
    padded = jnp.pad(fields, ((0, 0), (0, 0), (0, 0), (1, 1)))
    return filtered(fields, padded[..., 2:] + padded[..., :-2] - 2.0 * fields, diffraction)


def correlation(fields):
    return jnp.sum(fields[:, 0] * fields[:, 2] + fields[:, 1] * fields[:, 3], axis=0)


def section_pass(fields, slabs, active_planes, pulsation):
    diffraction = diffraction_of(pulsation)[:, None, None]
    images = []
    for depth_slot in range(slabs.shape[0]):
        updated = phase_shifted(fields, slabs[depth_slot], pulsation)
        padded = jnp.pad(updated, ((0, 0), (0, 0), (1, 1), (0, 0)))
        updated = filtered(updated, padded[:, :, 2:] + padded[:, :, :-2] - 2.0 * updated, diffraction)
        updated = across_columns(updated, diffraction)
        active_now = active_planes[depth_slot]
        fields = jnp.where(active_now > 0, updated, fields)
        images.append(active_now * correlation(updated) / fields.shape[0])
    return fields, jnp.stack(images)


def section_ticks(inputs):
    fields, slabs, active_planes, freqs = inputs
    return section_pass(fields, slabs, active_planes, angular_of(freqs))


def reference(waves_in, surface_waves, slowness, section_planes, block_freqs, surface_freqs):
    active_all = (jnp.arange(PLANES)[None, :] < section_planes[:, None]).astype(jnp.float32)
    first_out, first_image = lax.map(section_ticks, (waves_in, slowness, active_all, block_freqs))
    second_in = jnp.concatenate([surface_waves[None], first_out[:-1]], 0)
    second_freqs = jnp.concatenate([surface_freqs[None], block_freqs[:-1]], 0)
    waves_out, second_image = lax.map(section_ticks, (second_in, slowness, active_all, second_freqs))
    return waves_out, first_image + second_image
```

```python
import functools
import math

import jax
import jax.numpy as jnp
from jax import lax
from jax.experimental import pallas as pl
from jax.experimental.pallas import tpu as pltpu
from jax.sharding import PartitionSpec as P

DEPTH_STEP = 0.02
SMOOTHING = 0.4
BASE_HERTZ = 8.0
HERTZ_STEP = 0.5
DIFFRACTION_TOP = 0.2
MIDDLE_SLOWNESS = 0.445
SIN = (0.9999999998446159, -0.16666666052254658, 0.008333294444188614, -0.0001983264692424553, 2.6775178137139403e-06)
COS = (0.9999999982977188, -0.4999999326780431, 0.04166624044803908, -0.0013879434435051892, 2.394331932466174e-05)
SUB, LANE = 8, 128
TILE = (SUB, LANE)


def horner(coefficients, t):
    value = coefficients[-1] * t + coefficients[-2]
    for c in coefficients[-3::-1]:
        value = value * t + c
    return value


def sin_cos(x):
    t = x * x
    return x * horner(SIN, t), horner(COS, t)


def constants_of(omega):
    beta = DIFFRACTION_TOP * (2.0 * math.pi * BASE_HERTZ) / omega
    rate = omega * DEPTH_STEP
    half_sin, half_cos = sin_cos(rate * (0.5 * MIDDLE_SLOWNESS))
    centre_sin, centre_cos = 2.0 * half_sin * half_cos, 1.0 - 2.0 * half_sin * half_sin
    norm = SMOOTHING * SMOOTHING + beta * beta
    g_re, g_im = SMOOTHING / norm - 2.0, -beta / norm
    a_re, a_im = SMOOTHING * SMOOTHING - beta * beta, 2.0 * SMOOTHING * beta
    k_re = a_re * centre_cos - a_im * centre_sin
    k_im = a_re * centre_sin + a_im * centre_cos
    return rate, g_re, g_im, k_re, k_im


def kernel(
    axes, waves, surface, slowness, planes_ref, freqs, surface_freqs, waves_out, image_out,
    nat, nat_surface, nat_slow, window, window2, slow, states, outgoing, omegas, omegas2, image, nat_out, nat_image,
    in_sem, out_sem, slow_send, slow_recv, halo_send, halo_recv, depth_send, depth_recv, omega_sem,
):
    sections, strips = axes
    s, l = lax.axis_index("depth"), lax.axis_index("lat")
    fb, plane_count = waves.shape[1], slowness.shape[1]
    halo = plane_count
    strip = waves.shape[3]
    folded = strips == 2
    top = 0 if folded else halo
    width = top + strip + halo
    following, previous = {"depth": lax.rem(s + 1, sections)}, {"depth": lax.rem(s + sections - 1, sections)}
    has_next, has_previous = s < sections - 1, s > 0

    if folded:
        other = {"lat": 1 - l}
        sides = [(None, None, other, [(strip - 1 - i, strip + i, 1) for i in range(halo)])]
    else:
        down, up = {"lat": lax.rem(l + 1, strips)}, {"lat": lax.rem(l + strips - 1, strips)}
        sides = [
            (l < strips - 1, l > 0, down, [(top + strip - halo, 0, halo)]),
            (l > 0, l < strips - 1, up, [(top, top + strip, halo)]),
        ]

    def run_if(condition, body):
        if condition is None:
            body()
        else:
            pl.when(condition)(body)

    def halo_copies(source, target, send, recv, partner, copies, first):
        return [
            pltpu.make_async_remote_copy(
                src_ref=source.at[pl.ds(row, rows)], dst_ref=target.at[pl.ds(place, rows)],
                send_sem=send.at[first + i], recv_sem=recv.at[first + i],
                device_id=partner, device_id_type=pl.DeviceIdType.MESH,
            )
            for i, (row, place, rows) in enumerate(copies)
        ]

    def halos(buffer, send, recv, action):
        first = 0
        for can_send, can_receive, partner, copies in sides:
            descriptors = halo_copies(buffer, buffer, send, recv, partner, copies, first)
            first += len(copies)

            def act(descriptors=descriptors):
                for copy in descriptors:
                    getattr(copy, action)()

            run_if(can_receive if action == "wait_recv" else can_send, act)

    def place_of(i):
        return i + l * (strip - 1 - 2 * i) if folded else i

    def natural(source, target, send, inward):
        copies = []
        for t in range(SUB):
            far = source.at[:, :, pl.ds(t * LANE, LANE)]
            near = target.at[:, pl.ds(t * strip, strip), :]
            copies.append(pltpu.make_async_copy(far, near, send.at[t]) if inward else pltpu.make_async_copy(near, far, send.at[t]))
        return copies

    def waves_copies(f):
        return natural(waves.at[0, f], nat.at[pl.ds(f * 4, 4)], in_sem.at[0, f], True)

    def surface_copies(f):
        return natural(surface.at[f], nat_surface.at[pl.ds(f * 4, 4)], in_sem.at[1, f], True)

    slow_copies = natural(slowness.at[0], nat_slow, in_sem.at[2, 0], True)
    for copy in slow_copies:
        copy.start()
    for f in range(fb):
        for copy in waves_copies(f):
            copy.start()

    @pl.when(s == 0)
    def _():
        for f in range(fb):
            for copy in surface_copies(f):
                copy.start()

    barrier = pltpu.get_barrier_semaphore()

    def greet(partner):
        pl.semaphore_signal(barrier, inc=1, device_id=partner, device_id_type=pl.DeviceIdType.MESH)

    for can_send, _, partner, _ in sides:
        run_if(can_send, functools.partial(greet, partner))
    run_if(has_next, functools.partial(greet, following))
    run_if(has_previous, functools.partial(greet, previous))

    def omega_tile(k):
        return jnp.full(TILE, 2.0 * math.pi * (BASE_HERTZ + HERTZ_STEP * k.astype(jnp.float32)), jnp.float32)

    for f in range(fb):
        omegas[f] = omega_tile(freqs[0, f])
    image[...] = jnp.zeros_like(image)
    if not folded:
        for f in range(fb):
            for buffer in (window, window2):
                buffer[f, :top] = jnp.zeros_like(buffer[f, :top])
                buffer[f, top + strip :] = jnp.zeros_like(buffer[f, top + strip :])
        slow[:top] = jnp.zeros_like(slow[:top])
        slow[top + strip :] = jnp.zeros_like(slow[top + strip :])
    for copy in slow_copies:
        copy.wait()
    for p in range(plane_count):
        for i in range(strip):
            slow[top + i, p] = nat_slow[p, pl.ds(place_of(i), SUB, stride=strip), :]

    peers = jnp.where(has_next, 1, 0) + jnp.where(has_previous, 1, 0)
    for can_send, _, _, _ in sides:
        peers = peers + (1 if can_send is None else jnp.where(can_send, 1, 0))
    pl.semaphore_wait(barrier, peers)

    omega_copy = pltpu.make_async_remote_copy(
        src_ref=omegas, dst_ref=omegas2, send_sem=omega_sem.at[0], recv_sem=omega_sem.at[1],
        device_id=following, device_id_type=pl.DeviceIdType.MESH,
    )
    halos(slow, slow_send, slow_recv, "start")
    run_if(has_next, omega_copy.start)

    def relayout(source, target, f):
        for i in range(strip):
            for c in range(4):
                target[f, top + i, c] = source[f * 4 + c, pl.ds(place_of(i), SUB, stride=strip), :]

    @pl.loop(0, fb)
    def _(f):
        for copy in waves_copies(f):
            copy.wait()
        relayout(nat, window, f)
        halos(window.at[f], halo_send.at[0, f], halo_recv.at[0, f], "start")

    row_of = lax.broadcasted_iota(jnp.int32, TILE, 0)
    lane_of = lax.broadcasted_iota(jnp.int32, TILE, 1)
    first_lane, last_lane = lane_of == 0, lane_of == LANE - 1
    first_row, last_row = row_of == 0, row_of == SUB - 1

    def beside(u):
        left = pltpu.roll(u, 1, 1)
        right = pltpu.roll(u, LANE - 1, 1)
        before = jnp.where(first_row, 0.0, pltpu.roll(left, 1, 0))
        after = jnp.where(last_row, 0.0, pltpu.roll(right, SUB - 1, 0))
        return jnp.where(first_lane, before, left) + jnp.where(last_lane, after, right)

    def section(load, omega):
        rate, g_re, g_im, k_re, k_im = constants_of(omega)

        def spread(u, total):
            s_re, s_im, r_re, r_im = u
            return (
                g_re * s_re - g_im * s_im + total[0],
                g_re * s_im + g_im * s_re + total[1],
                g_re * r_re + g_im * r_im + total[2],
                g_re * r_im - g_im * r_re + total[3],
            )

        def rotated(p, j):
            sin, cos = sin_cos((slow[j, p] - MIDDLE_SLOWNESS) * rate)
            e_re, e_im = k_re * cos - k_im * sin, k_re * sin + k_im * cos
            s_re, s_im, r_re, r_im = [load(j, c) if p == 0 else states[p - 1, j, c] for c in range(4)]
            return (
                s_re * e_re - s_im * e_im,
                s_re * e_im + s_im * e_re,
                r_re * e_re + r_im * e_im,
                r_im * e_re - r_re * e_im,
            )

        for p in range(plane_count):
            low, high = (0 if folded else p + 1), width - 1 - p
            behind = None if folded else rotated(p, low - 1)
            here = rotated(p, low)
            for j in range(low, high):
                ahead = rotated(p, j + 1)
                total = ahead if behind is None else [x + y for x, y in zip(behind, ahead)]
                u = spread(here, total)
                if j < top:
                    u = [jnp.where(l > 0, x, 0.0) for x in u]
                elif j >= top + strip and not folded:
                    u = [jnp.where(l < strips - 1, x, 0.0) for x in u]
                u = spread(u, [beside(x) for x in u])
                for c in range(4):
                    states[p, j, c] = u[c]
                if top <= j < top + strip:
                    image[p, j - top] += u[0] * u[2] + u[1] * u[3]
                behind, here = here, ahead

    last_plane = jnp.clip(planes_ref[0] - 1, 0, plane_count - 1)

    def depth_copy(f):
        return pltpu.make_async_remote_copy(
            src_ref=outgoing.at[f], dst_ref=window2.at[f, pl.ds(top, strip)],
            send_sem=depth_send.at[f], recv_sem=depth_recv.at[f],
            device_id=following, device_id_type=pl.DeviceIdType.MESH,
        )

    halos(slow, slow_send, slow_recv, "wait_recv")

    @pl.loop(0, fb)
    def _(f):
        halos(window.at[f], halo_send.at[0, f], halo_recv.at[0, f], "wait_recv")
        section(lambda j, c: window[f, j, c], omegas[f])
        for i in range(strip):
            for c in range(4):
                outgoing[f, i, c] = states[last_plane, top + i, c]

        @pl.when(has_next)
        def _():
            depth_copy(f).start()

    @pl.when(has_previous)
    def _():
        omega_copy.wait_recv()

    @pl.when(s == 0)
    def _():
        for f in range(fb):
            omegas2[f] = omega_tile(surface_freqs[f])

    def arrive(f):
        @pl.when(has_previous)
        def _():
            depth_copy(f).wait_recv()

        @pl.when(s == 0)
        def _():
            for copy in surface_copies(f):
                copy.wait()
            relayout(nat_surface, window2, f)

        halos(window2.at[f], halo_send.at[1, f], halo_recv.at[1, f], "start")

    def out_copies(f):
        return natural(waves_out.at[0, f], nat_out.at[pl.ds(f * 4, 4)], out_sem.at[f], False)

    arrive(0)

    @pl.loop(0, fb)
    def _(f):
        @pl.when(f < fb - 1)
        def _():
            arrive(f + 1)

        halos(window2.at[f], halo_send.at[1, f], halo_recv.at[1, f], "wait_recv")
        section(lambda j, c: window2[f, j, c], omegas2[f])
        for i in range(strip):
            for c in range(4):
                nat_out[f * 4 + c, pl.ds(place_of(i), SUB, stride=strip), :] = states[last_plane, top + i, c]
        for copy in out_copies(f):
            copy.start()

    for p in range(plane_count):
        weight = jnp.where(p <= last_plane, 1.0 / fb, 0.0)
        for i in range(strip):
            nat_image[p, pl.ds(place_of(i), SUB, stride=strip), :] = image[p, i] * weight
    image_copies = natural(image_out.at[0], nat_image, out_sem.at[fb], False)
    for copy in image_copies:
        copy.start()
    halos(slow, slow_send, slow_recv, "wait_send")

    @pl.when(has_next)
    def _():
        omega_copy.wait_send()
        for f in range(fb):
            depth_copy(f).wait_send()

    for f in range(fb):
        halos(window.at[f], halo_send.at[0, f], halo_recv.at[0, f], "wait_send")
        halos(window2.at[f], halo_send.at[1, f], halo_recv.at[1, f], "wait_send")
        for copy in out_copies(f):
            copy.wait()
    for copy in image_copies:
        copy.wait()


def local(waves_in, surface_waves, slowness, section_planes, block_freqs, surface_freqs):
    axes = (lax.axis_size("depth"), lax.axis_size("lat"))
    _, fb, _, strip, columns = waves_in.shape
    plane_count = slowness.shape[1]
    if columns != SUB * LANE or strip != SUB:
        raise ValueError("unsupported strip")
    folded = axes[1] == 2
    width = (0 if folded else plane_count) + strip + plane_count
    per_halo = plane_count if folded else 2
    f32 = jnp.float32
    dma = pltpu.SemaphoreType.DMA
    anywhere = pl.BlockSpec(memory_space=pl.ANY)
    scalars = pl.BlockSpec(memory_space=pltpu.SMEM)
    return pl.pallas_call(
        functools.partial(kernel, axes),
        out_shape=(jax.ShapeDtypeStruct(waves_in.shape, f32), jax.ShapeDtypeStruct(slowness.shape, f32)),
        in_specs=[anywhere] * 3 + [scalars] * 3,
        out_specs=(anywhere, anywhere),
        scratch_shapes=[
            pltpu.VMEM((fb * 4, SUB * strip, LANE), f32),
            pltpu.VMEM((fb * 4, SUB * strip, LANE), f32),
            pltpu.VMEM((plane_count, SUB * strip, LANE), f32),
            pltpu.VMEM((fb, width, 4) + TILE, f32),
            pltpu.VMEM((fb, width, 4) + TILE, f32),
            pltpu.VMEM((width, plane_count) + TILE, f32),
            pltpu.VMEM((plane_count, width, 4) + TILE, f32),
            pltpu.VMEM((fb, strip, 4) + TILE, f32),
            pltpu.VMEM((fb,) + TILE, f32),
            pltpu.VMEM((fb,) + TILE, f32),
            pltpu.VMEM((plane_count, strip) + TILE, f32),
            pltpu.VMEM((fb * 4, SUB * strip, LANE), f32),
            pltpu.VMEM((plane_count, SUB * strip, LANE), f32),
            dma((3, fb, SUB)),
            dma((fb + 1, SUB)),
            dma((per_halo,)),
            dma((per_halo,)),
            dma((2, fb, per_halo)),
            dma((2, fb, per_halo)),
            dma((fb,)),
            dma((fb,)),
            dma((2,)),
        ],
        compiler_params=pltpu.CompilerParams(collective_id=0, has_side_effects=True),
        name="migrate",
    )(waves_in, surface_waves, slowness, section_planes, block_freqs, surface_freqs)


def solution(mesh):
    return jax.shard_map(
        local,
        mesh=mesh,
        in_specs=(
            P("depth", None, None, "lat", None),
            P(None, None, "lat", None),
            P("depth", None, "lat", None),
            P("depth"),
            P("depth", None),
            P(),
        ),
        out_specs=(P("depth", None, None, "lat", None), P("depth", None, "lat", None)),
        check_vma=False,
    )
```

```python
import functools
import math

import jax
import jax.numpy as jnp
from jax import lax
from jax.experimental import pallas as pl
from jax.experimental.pallas import tpu as pltpu
from jax.sharding import PartitionSpec as P

DEPTH_STEP = 0.02
SMOOTHING = 0.4
BASE_HERTZ = 8.0
HERTZ_STEP = 0.5
DIFFRACTION_TOP = 0.2
MIDDLE_SLOWNESS = 0.445
SIN = (0.9999999998446159, -0.16666666052254658, 0.008333294444188614, -0.0001983264692424553, 2.6775178137139403e-06)
COS = (0.9999999982977188, -0.4999999326780431, 0.04166624044803908, -0.0013879434435051892, 2.394331932466174e-05)
SUB, LANE = 8, 128
TILE = (SUB, LANE)


def horner(coefficients, t):
    value = coefficients[-1] * t + coefficients[-2]
    for c in coefficients[-3::-1]:
        value = value * t + c
    return value


def sin_cos(x):
    t = x * x
    return x * horner(SIN, t), horner(COS, t)


def constants_of(omega):
    beta = DIFFRACTION_TOP * (2.0 * math.pi * BASE_HERTZ) / omega
    rate = omega * DEPTH_STEP
    half_sin, half_cos = sin_cos(rate * (0.5 * MIDDLE_SLOWNESS))
    centre_sin, centre_cos = 2.0 * half_sin * half_cos, 1.0 - 2.0 * half_sin * half_sin
    norm = SMOOTHING * SMOOTHING + beta * beta
    g_re, g_im = SMOOTHING / norm - 2.0, -beta / norm
    a_re, a_im = SMOOTHING * SMOOTHING - beta * beta, 2.0 * SMOOTHING * beta
    k_re = a_re * centre_cos - a_im * centre_sin
    k_im = a_re * centre_sin + a_im * centre_cos
    return rate, g_re, g_im, k_re, k_im


def kernel(
    axes, waves, surface, slowness, planes_ref, freqs, surface_freqs, waves_out, image_out,
    nat, nat_surface, nat_slow, window, window2, slow, states, outgoing, omegas, omegas2, image, nat_out, nat_image,
    in_sem, out_sem, slow_send, slow_recv, halo_send, halo_recv, depth_send, depth_recv, omega_sem,
):
    sections, strips = axes
    s, l = lax.axis_index("depth"), lax.axis_index("lat")
    fb, plane_count = waves.shape[1], slowness.shape[1]
    halo = plane_count
    strip = waves.shape[3]
    folded = strips == 2
    top = 0 if folded else halo
    width = top + strip + halo
    following, previous = {"depth": lax.rem(s + 1, sections)}, {"depth": lax.rem(s + sections - 1, sections)}
    has_next, has_previous = s < sections - 1, s > 0

    if folded:
        other = {"lat": 1 - l}
        sides = [(None, None, other, [(strip - 1 - i, strip + i, 1) for i in range(halo)])]
    else:
        down, up = {"lat": lax.rem(l + 1, strips)}, {"lat": lax.rem(l + strips - 1, strips)}
        sides = [
            (l < strips - 1, l > 0, down, [(top + strip - halo, 0, halo)]),
            (l > 0, l < strips - 1, up, [(top, top + strip, halo)]),
        ]

    def run_if(condition, body):
        if condition is None:
            body()
        else:
            pl.when(condition)(body)

    def halo_copies(buffer, send, recv, partner, copies, first, trimmed):
        def view(row, rows, i):
            return buffer.at[pl.ds(row, rows), pl.ds(0, plane_count - i)] if trimmed and folded else buffer.at[pl.ds(row, rows)]

        return [
            pltpu.make_async_remote_copy(
                src_ref=view(row, rows, i), dst_ref=view(place, rows, i),
                send_sem=send.at[first + i], recv_sem=recv.at[first + i],
                device_id=partner, device_id_type=pl.DeviceIdType.MESH,
            )
            for i, (row, place, rows) in enumerate(copies)
        ]

    def halos(buffer, send, recv, action, trimmed=False):
        first = 0
        for can_send, can_receive, partner, copies in sides:
            descriptors = halo_copies(buffer, send, recv, partner, copies, first, trimmed)
            first += len(copies)

            def act(descriptors=descriptors):
                for copy in descriptors:
                    getattr(copy, action)()

            run_if(can_receive if action == "wait_recv" else can_send, act)

    def place_of(i):
        return i + l * (strip - 1 - 2 * i) if folded else i

    def natural(source, target, send, inward):
        copies = []
        for t in range(SUB):
            far = source.at[:, :, pl.ds(t * LANE, LANE)]
            near = target.at[:, pl.ds(t * strip, strip), :]
            copies.append(pltpu.make_async_copy(far, near, send.at[t]) if inward else pltpu.make_async_copy(near, far, send.at[t]))
        return copies

    def waves_copies(f):
        return natural(waves.at[0, f], nat.at[pl.ds(f * 4, 4)], in_sem.at[0, f], True)

    def surface_copies(f):
        return natural(surface.at[f], nat_surface.at[pl.ds(f * 4, 4)], in_sem.at[1, f], True)

    slow_copies = natural(slowness.at[0], nat_slow, in_sem.at[2, 0], True)
    for copy in slow_copies:
        copy.start()
    for f in range(fb):
        for copy in waves_copies(f):
            copy.start()

    @pl.when(s == 0)
    def _():
        for f in range(fb):
            for copy in surface_copies(f):
                copy.start()

    barrier = pltpu.get_barrier_semaphore()

    def greet(partner):
        pl.semaphore_signal(barrier, inc=1, device_id=partner, device_id_type=pl.DeviceIdType.MESH)

    for can_send, _, partner, _ in sides:
        run_if(can_send, functools.partial(greet, partner))
    run_if(has_next, functools.partial(greet, following))
    run_if(has_previous, functools.partial(greet, previous))

    def omega_tile(k):
        return jnp.full(TILE, 2.0 * math.pi * (BASE_HERTZ + HERTZ_STEP * k.astype(jnp.float32)), jnp.float32)

    for f in range(fb):
        omegas[f] = omega_tile(freqs[0, f])
    image[...] = jnp.zeros_like(image)
    if not folded:
        for f in range(fb):
            for buffer in (window, window2):
                buffer[f, :top] = jnp.zeros_like(buffer[f, :top])
                buffer[f, top + strip :] = jnp.zeros_like(buffer[f, top + strip :])
        slow[:top] = jnp.zeros_like(slow[:top])
        slow[top + strip :] = jnp.zeros_like(slow[top + strip :])
    for copy in slow_copies:
        copy.wait()
    for p in range(plane_count):
        for i in range(strip):
            slow[top + i, p] = nat_slow[p, pl.ds(place_of(i), SUB, stride=strip), :]

    peers = jnp.where(has_next, 1, 0) + jnp.where(has_previous, 1, 0)
    for can_send, _, _, _ in sides:
        peers = peers + (1 if can_send is None else jnp.where(can_send, 1, 0))
    pl.semaphore_wait(barrier, peers)

    omega_copy = pltpu.make_async_remote_copy(
        src_ref=omegas, dst_ref=omegas2, send_sem=omega_sem.at[0], recv_sem=omega_sem.at[1],
        device_id=following, device_id_type=pl.DeviceIdType.MESH,
    )
    halos(slow, slow_send, slow_recv, "start", True)
    run_if(has_next, omega_copy.start)

    def relayout(source, target, f):
        for i in range(strip):
            for c in range(4):
                target[f, top + i, c] = source[f * 4 + c, pl.ds(place_of(i), SUB, stride=strip), :]

    @pl.loop(0, fb)
    def _(f):
        for copy in waves_copies(f):
            copy.wait()
        relayout(nat, window, f)
        halos(window.at[f], halo_send.at[0, f], halo_recv.at[0, f], "start")

    row_of = lax.broadcasted_iota(jnp.int32, TILE, 0)
    lane_of = lax.broadcasted_iota(jnp.int32, TILE, 1)
    first_lane, last_lane = lane_of == 0, lane_of == LANE - 1
    first_row, last_row = row_of == 0, row_of == SUB - 1

    def beside(u):
        left = pltpu.roll(u, 1, 1)
        right = pltpu.roll(u, LANE - 1, 1)
        before = jnp.where(first_row, 0.0, pltpu.roll(left, 1, 0))
        after = jnp.where(last_row, 0.0, pltpu.roll(right, SUB - 1, 0))
        return jnp.where(first_lane, before, left) + jnp.where(last_lane, after, right)

    def section(load, omega):
        rate, g_re, g_im, k_re, k_im = constants_of(omega)

        def spread(u, total):
            s_re, s_im, r_re, r_im = u
            return (
                g_re * s_re - g_im * s_im + total[0],
                g_re * s_im + g_im * s_re + total[1],
                g_re * r_re + g_im * r_im + total[2],
                g_re * r_im - g_im * r_re + total[3],
            )

        def rotated(p, j):
            sin, cos = sin_cos((slow[j, p] - MIDDLE_SLOWNESS) * rate)
            e_re, e_im = k_re * cos - k_im * sin, k_re * sin + k_im * cos
            s_re, s_im, r_re, r_im = [load(j, c) if p == 0 else states[p - 1, j, c] for c in range(4)]
            return (
                s_re * e_re - s_im * e_im,
                s_re * e_im + s_im * e_re,
                r_re * e_re + r_im * e_im,
                r_im * e_re - r_re * e_im,
            )

        for p in range(plane_count):
            low, high = (0 if folded else p + 1), width - 1 - p
            behind = None if folded else rotated(p, low - 1)
            here = rotated(p, low)
            for j in range(low, high):
                ahead = rotated(p, j + 1)
                total = ahead if behind is None else [x + y for x, y in zip(behind, ahead)]
                u = spread(here, total)
                if j < top:
                    u = [jnp.where(l > 0, x, 0.0) for x in u]
                elif j >= top + strip and not folded:
                    u = [jnp.where(l < strips - 1, x, 0.0) for x in u]
                u = spread(u, [beside(x) for x in u])
                for c in range(4):
                    states[p, j, c] = u[c]
                if top <= j < top + strip:
                    image[p, j - top] += u[0] * u[2] + u[1] * u[3]
                behind, here = here, ahead

    last_plane = jnp.clip(planes_ref[0] - 1, 0, plane_count - 1)

    def depth_copy(f):
        return pltpu.make_async_remote_copy(
            src_ref=outgoing.at[f], dst_ref=window2.at[f, pl.ds(top, strip)],
            send_sem=depth_send.at[f], recv_sem=depth_recv.at[f],
            device_id=following, device_id_type=pl.DeviceIdType.MESH,
        )

    halos(slow, slow_send, slow_recv, "wait_recv", True)

    @pl.loop(0, fb)
    def _(f):
        halos(window.at[f], halo_send.at[0, f], halo_recv.at[0, f], "wait_recv")
        section(lambda j, c: window[f, j, c], omegas[f])
        for i in range(strip):
            for c in range(4):
                outgoing[f, i, c] = states[last_plane, top + i, c]

        @pl.when(has_next)
        def _():
            depth_copy(f).start()

    @pl.when(has_previous)
    def _():
        omega_copy.wait_recv()

    @pl.when(s == 0)
    def _():
        for f in range(fb):
            omegas2[f] = omega_tile(surface_freqs[f])

    def arrive(f):
        @pl.when(has_previous)
        def _():
            depth_copy(f).wait_recv()

        @pl.when(s == 0)
        def _():
            for copy in surface_copies(f):
                copy.wait()
            relayout(nat_surface, window2, f)

        halos(window2.at[f], halo_send.at[1, f], halo_recv.at[1, f], "start")

    def out_copies(f):
        return natural(waves_out.at[0, f], nat_out.at[pl.ds(f * 4, 4)], out_sem.at[f], False)

    arrive(0)

    @pl.loop(0, fb)
    def _(f):
        @pl.when(f < fb - 1)
        def _():
            arrive(f + 1)

        halos(window2.at[f], halo_send.at[1, f], halo_recv.at[1, f], "wait_recv")
        section(lambda j, c: window2[f, j, c], omegas2[f])
        for i in range(strip):
            for c in range(4):
                nat_out[f * 4 + c, pl.ds(place_of(i), SUB, stride=strip), :] = states[last_plane, top + i, c]
        for copy in out_copies(f):
            copy.start()

    for p in range(plane_count):
        weight = jnp.where(p <= last_plane, 1.0 / fb, 0.0)
        for i in range(strip):
            nat_image[p, pl.ds(place_of(i), SUB, stride=strip), :] = image[p, i] * weight
    image_copies = natural(image_out.at[0], nat_image, out_sem.at[fb], False)
    for copy in image_copies:
        copy.start()
    halos(slow, slow_send, slow_recv, "wait_send", True)

    @pl.when(has_next)
    def _():
        omega_copy.wait_send()
        for f in range(fb):
            depth_copy(f).wait_send()

    for f in range(fb):
        halos(window.at[f], halo_send.at[0, f], halo_recv.at[0, f], "wait_send")
        halos(window2.at[f], halo_send.at[1, f], halo_recv.at[1, f], "wait_send")
        for copy in out_copies(f):
            copy.wait()
    for copy in image_copies:
        copy.wait()


def local(waves_in, surface_waves, slowness, section_planes, block_freqs, surface_freqs):
    axes = (lax.axis_size("depth"), lax.axis_size("lat"))
    _, fb, _, strip, columns = waves_in.shape
    plane_count = slowness.shape[1]
    if columns != SUB * LANE or strip != SUB:
        raise ValueError("unsupported strip")
    folded = axes[1] == 2
    width = (0 if folded else plane_count) + strip + plane_count
    per_halo = plane_count if folded else 2
    f32 = jnp.float32
    dma = pltpu.SemaphoreType.DMA
    anywhere = pl.BlockSpec(memory_space=pl.ANY)
    scalars = pl.BlockSpec(memory_space=pltpu.SMEM)
    return pl.pallas_call(
        functools.partial(kernel, axes),
        out_shape=(jax.ShapeDtypeStruct(waves_in.shape, f32), jax.ShapeDtypeStruct(slowness.shape, f32)),
        in_specs=[pl.BlockSpec(memory_space=pltpu.HBM)] * 3 + [scalars] * 3,
        out_specs=(anywhere, anywhere),
        scratch_shapes=[
            pltpu.VMEM((fb * 4, SUB * strip, LANE), f32),
            pltpu.VMEM((fb * 4, SUB * strip, LANE), f32),
            pltpu.VMEM((plane_count, SUB * strip, LANE), f32),
            pltpu.VMEM((fb, width, 4) + TILE, f32),
            pltpu.VMEM((fb, width, 4) + TILE, f32),
            pltpu.VMEM((width, plane_count) + TILE, f32),
            pltpu.VMEM((plane_count, width, 4) + TILE, f32),
            pltpu.VMEM((fb, strip, 4) + TILE, f32),
            pltpu.VMEM((fb,) + TILE, f32),
            pltpu.VMEM((fb,) + TILE, f32),
            pltpu.VMEM((plane_count, strip) + TILE, f32),
            pltpu.VMEM((fb * 4, SUB * strip, LANE), f32),
            pltpu.VMEM((plane_count, SUB * strip, LANE), f32),
            dma((3, fb, SUB)),
            dma((fb + 1, SUB)),
            dma((per_halo,)),
            dma((per_halo,)),
            dma((2, fb, per_halo)),
            dma((2, fb, per_halo)),
            dma((fb,)),
            dma((fb,)),
            dma((2,)),
        ],
        compiler_params=pltpu.CompilerParams(collective_id=0, has_side_effects=True, vmem_limit_bytes=32 << 20),
        name="migrate",
    )(waves_in, surface_waves, slowness, section_planes, block_freqs, surface_freqs)


def solution(mesh):
    return jax.shard_map(
        local,
        mesh=mesh,
        in_specs=(
            P("depth", None, None, "lat", None),
            P(None, None, "lat", None),
            P("depth", None, "lat", None),
            P("depth"),
            P("depth", None),
            P(),
        ),
        out_specs=(P("depth", None, None, "lat", None), P("depth", None, "lat", None)),
        check_vma=False,
    )
```

```python
import functools
import math

import jax
import jax.numpy as jnp
from jax import lax
from jax.experimental import pallas as pl
from jax.experimental.pallas import tpu as pltpu
from jax.sharding import PartitionSpec as P

DEPTH_STEP = 0.02
SMOOTHING = 0.4
BASE_HERTZ = 8.0
HERTZ_STEP = 0.5
DIFFRACTION_TOP = 0.2
MIDDLE_SLOWNESS = 0.445
SIN = (0.9999999998446159, -0.16666666052254658, 0.008333294444188614, -0.0001983264692424553, 2.6775178137139403e-06)
COS = (0.9999999982977188, -0.4999999326780431, 0.04166624044803908, -0.0013879434435051892, 2.394331932466174e-05)
SUB, LANE = 8, 128
TILE = (SUB, LANE)


def horner(coefficients, t):
    value = coefficients[-1] * t + coefficients[-2]
    for c in coefficients[-3::-1]:
        value = value * t + c
    return value


def sin_cos(x):
    t = x * x
    return x * horner(SIN, t), horner(COS, t)


def constants_of(omega):
    beta = DIFFRACTION_TOP * (2.0 * math.pi * BASE_HERTZ) / omega
    rate = omega * DEPTH_STEP
    half_sin, half_cos = sin_cos(rate * (0.5 * MIDDLE_SLOWNESS))
    centre_sin, centre_cos = 2.0 * half_sin * half_cos, 1.0 - 2.0 * half_sin * half_sin
    norm = SMOOTHING * SMOOTHING + beta * beta
    g_re, g_im = SMOOTHING / norm - 2.0, -beta / norm
    a_re, a_im = SMOOTHING * SMOOTHING - beta * beta, 2.0 * SMOOTHING * beta
    k_re = a_re * centre_cos - a_im * centre_sin
    k_im = a_re * centre_sin + a_im * centre_cos
    return rate, g_re, g_im, k_re, k_im


def kernel(
    axes, waves, surface, slowness, planes_ref, freqs, surface_freqs, nat_out, nat_image,
    nat, nat_surface, nat_slow, window, window2, slow, states, outgoing, omegas, omegas2, image,
    in_sem, slow_send, slow_recv, halo_send, halo_recv, depth_send, depth_recv, omega_sem,
):
    sections, strips = axes
    s, l = lax.axis_index("depth"), lax.axis_index("lat")
    fb, plane_count = waves.shape[1], slowness.shape[1]
    halo = plane_count
    strip = waves.shape[3]
    folded = strips == 2
    top = 0 if folded else halo
    width = top + strip + halo
    following, previous = {"depth": lax.rem(s + 1, sections)}, {"depth": lax.rem(s + sections - 1, sections)}
    has_next, has_previous = s < sections - 1, s > 0

    if folded:
        other = {"lat": 1 - l}
        sides = [(None, None, other, [(strip - 1 - i, strip + i, 1) for i in range(halo)])]
    else:
        down, up = {"lat": lax.rem(l + 1, strips)}, {"lat": lax.rem(l + strips - 1, strips)}
        sides = [
            (l < strips - 1, l > 0, down, [(top + strip - halo, 0, halo)]),
            (l > 0, l < strips - 1, up, [(top, top + strip, halo)]),
        ]

    def run_if(condition, body):
        if condition is None:
            body()
        else:
            pl.when(condition)(body)

    def halo_copies(buffer, send, recv, partner, copies, first, trimmed):
        def view(row, rows, i):
            return buffer.at[pl.ds(row, rows), pl.ds(0, plane_count - i)] if trimmed and folded else buffer.at[pl.ds(row, rows)]

        return [
            pltpu.make_async_remote_copy(
                src_ref=view(row, rows, i), dst_ref=view(place, rows, i),
                send_sem=send.at[first + i], recv_sem=recv.at[first + i],
                device_id=partner, device_id_type=pl.DeviceIdType.MESH,
            )
            for i, (row, place, rows) in enumerate(copies)
        ]

    def halos(buffer, send, recv, action, trimmed=False):
        first = 0
        for can_send, can_receive, partner, copies in sides:
            descriptors = halo_copies(buffer, send, recv, partner, copies, first, trimmed)
            first += len(copies)

            def act(descriptors=descriptors):
                for copy in descriptors:
                    getattr(copy, action)()

            run_if(can_receive if action == "wait_recv" else can_send, act)

    def place_of(i):
        return i + l * (strip - 1 - 2 * i) if folded else i

    def natural(source, target, send):
        return [
            pltpu.make_async_copy(source.at[:, :, pl.ds(t * LANE, LANE)], target.at[:, pl.ds(t * strip, strip), :], send.at[t])
            for t in range(SUB)
        ]

    def waves_copies(f):
        return natural(waves.at[0, f], nat.at[pl.ds(f * 4, 4)], in_sem.at[0, f])

    def surface_copies(f):
        return natural(surface.at[f], nat_surface.at[pl.ds(f * 4, 4)], in_sem.at[1, f])

    slow_copies = natural(slowness.at[0], nat_slow, in_sem.at[2, 0])
    for copy in slow_copies:
        copy.start()
    for f in range(fb):
        for copy in waves_copies(f):
            copy.start()

    @pl.when(s == 0)
    def _():
        for f in range(fb):
            for copy in surface_copies(f):
                copy.start()

    barrier = pltpu.get_barrier_semaphore()

    def greet(partner):
        pl.semaphore_signal(barrier, inc=1, device_id=partner, device_id_type=pl.DeviceIdType.MESH)

    for can_send, _, partner, _ in sides:
        run_if(can_send, functools.partial(greet, partner))
    run_if(has_next, functools.partial(greet, following))
    run_if(has_previous, functools.partial(greet, previous))

    def omega_tile(k):
        return jnp.full(TILE, 2.0 * math.pi * (BASE_HERTZ + HERTZ_STEP * k.astype(jnp.float32)), jnp.float32)

    for f in range(fb):
        omegas[f] = omega_tile(freqs[0, f])
    image[...] = jnp.zeros_like(image)
    if not folded:
        for f in range(fb):
            for buffer in (window, window2):
                buffer[f, :top] = jnp.zeros_like(buffer[f, :top])
                buffer[f, top + strip :] = jnp.zeros_like(buffer[f, top + strip :])
        slow[:top] = jnp.zeros_like(slow[:top])
        slow[top + strip :] = jnp.zeros_like(slow[top + strip :])
    for copy in slow_copies:
        copy.wait()
    for p in range(plane_count):
        for i in range(strip):
            slow[top + i, p] = nat_slow[p, pl.ds(place_of(i), SUB, stride=strip), :]

    peers = jnp.where(has_next, 1, 0) + jnp.where(has_previous, 1, 0)
    for can_send, _, _, _ in sides:
        peers = peers + (1 if can_send is None else jnp.where(can_send, 1, 0))
    pl.semaphore_wait(barrier, peers)

    omega_copy = pltpu.make_async_remote_copy(
        src_ref=omegas, dst_ref=omegas2, send_sem=omega_sem.at[0], recv_sem=omega_sem.at[1],
        device_id=following, device_id_type=pl.DeviceIdType.MESH,
    )
    halos(slow, slow_send, slow_recv, "start", True)
    run_if(has_next, omega_copy.start)

    def relayout(source, target, f):
        for i in range(strip):
            for c in range(4):
                target[f, top + i, c] = source[f * 4 + c, pl.ds(place_of(i), SUB, stride=strip), :]

    @pl.loop(0, fb)
    def _(f):
        for copy in waves_copies(f):
            copy.wait()
        relayout(nat, window, f)
        halos(window.at[f], halo_send.at[0, f], halo_recv.at[0, f], "start")

    row_of = lax.broadcasted_iota(jnp.int32, TILE, 0)
    lane_of = lax.broadcasted_iota(jnp.int32, TILE, 1)
    first_lane, last_lane = lane_of == 0, lane_of == LANE - 1
    first_row, last_row = row_of == 0, row_of == SUB - 1

    def beside(u):
        left = pltpu.roll(u, 1, 1)
        right = pltpu.roll(u, LANE - 1, 1)
        before = jnp.where(first_row, 0.0, pltpu.roll(left, 1, 0))
        after = jnp.where(last_row, 0.0, pltpu.roll(right, SUB - 1, 0))
        return jnp.where(first_lane, before, left) + jnp.where(last_lane, after, right)

    def section(load, omega):
        rate, g_re, g_im, k_re, k_im = constants_of(omega)

        def spread(u, total):
            s_re, s_im, r_re, r_im = u
            return (
                g_re * s_re - g_im * s_im + total[0],
                g_re * s_im + g_im * s_re + total[1],
                g_re * r_re + g_im * r_im + total[2],
                g_re * r_im - g_im * r_re + total[3],
            )

        def rotated(p, j):
            sin, cos = sin_cos((slow[j, p] - MIDDLE_SLOWNESS) * rate)
            e_re, e_im = k_re * cos - k_im * sin, k_re * sin + k_im * cos
            s_re, s_im, r_re, r_im = [load(j, c) if p == 0 else states[p - 1, j, c] for c in range(4)]
            return (
                s_re * e_re - s_im * e_im,
                s_re * e_im + s_im * e_re,
                r_re * e_re + r_im * e_im,
                r_im * e_re - r_re * e_im,
            )

        for p in range(plane_count):
            low, high = (0 if folded else p + 1), width - 1 - p
            behind = None if folded else rotated(p, low - 1)
            here = rotated(p, low)
            for j in range(low, high):
                ahead = rotated(p, j + 1)
                total = ahead if behind is None else [x + y for x, y in zip(behind, ahead)]
                u = spread(here, total)
                if j < top:
                    u = [jnp.where(l > 0, x, 0.0) for x in u]
                elif j >= top + strip and not folded:
                    u = [jnp.where(l < strips - 1, x, 0.0) for x in u]
                u = spread(u, [beside(x) for x in u])
                for c in range(4):
                    states[p, j, c] = u[c]
                if top <= j < top + strip:
                    image[p, j - top] += u[0] * u[2] + u[1] * u[3]
                behind, here = here, ahead

    last_plane = jnp.clip(planes_ref[0] - 1, 0, plane_count - 1)

    def depth_copy(f):
        return pltpu.make_async_remote_copy(
            src_ref=outgoing.at[f], dst_ref=window2.at[f, pl.ds(top, strip)],
            send_sem=depth_send.at[f], recv_sem=depth_recv.at[f],
            device_id=following, device_id_type=pl.DeviceIdType.MESH,
        )

    halos(slow, slow_send, slow_recv, "wait_recv", True)

    @pl.loop(0, fb)
    def _(f):
        halos(window.at[f], halo_send.at[0, f], halo_recv.at[0, f], "wait_recv")
        section(lambda j, c: window[f, j, c], omegas[f])
        for i in range(strip):
            for c in range(4):
                outgoing[f, i, c] = states[last_plane, top + i, c]

        @pl.when(has_next)
        def _():
            depth_copy(f).start()

    @pl.when(has_previous)
    def _():
        omega_copy.wait_recv()

    @pl.when(s == 0)
    def _():
        for f in range(fb):
            omegas2[f] = omega_tile(surface_freqs[f])

    def arrive(f):
        @pl.when(has_previous)
        def _():
            depth_copy(f).wait_recv()

        @pl.when(s == 0)
        def _():
            for copy in surface_copies(f):
                copy.wait()
            relayout(nat_surface, window2, f)

        halos(window2.at[f], halo_send.at[1, f], halo_recv.at[1, f], "start")

    arrive(0)

    @pl.loop(0, fb)
    def _(f):
        @pl.when(f < fb - 1)
        def _():
            arrive(f + 1)

        halos(window2.at[f], halo_send.at[1, f], halo_recv.at[1, f], "wait_recv")
        section(lambda j, c: window2[f, j, c], omegas2[f])
        for i in range(strip):
            for c in range(4):
                nat_out[f * 4 + c, pl.ds(place_of(i), SUB, stride=strip), :] = states[last_plane, top + i, c]

    for p in range(plane_count):
        weight = jnp.where(p <= last_plane, 1.0 / fb, 0.0)
        for i in range(strip):
            nat_image[p, pl.ds(place_of(i), SUB, stride=strip), :] = image[p, i] * weight
    halos(slow, slow_send, slow_recv, "wait_send", True)

    @pl.when(has_next)
    def _():
        omega_copy.wait_send()
        for f in range(fb):
            depth_copy(f).wait_send()

    for f in range(fb):
        halos(window.at[f], halo_send.at[0, f], halo_recv.at[0, f], "wait_send")
        halos(window2.at[f], halo_send.at[1, f], halo_recv.at[1, f], "wait_send")


def local(waves_in, surface_waves, slowness, section_planes, block_freqs, surface_freqs):
    axes = (lax.axis_size("depth"), lax.axis_size("lat"))
    _, fb, _, strip, columns = waves_in.shape
    plane_count = slowness.shape[1]
    if columns != SUB * LANE or strip != SUB:
        raise ValueError("unsupported strip")
    folded = axes[1] == 2
    width = (0 if folded else plane_count) + strip + plane_count
    per_halo = plane_count if folded else 2
    f32 = jnp.float32
    dma = pltpu.SemaphoreType.DMA
    anywhere = pl.BlockSpec(memory_space=pl.ANY)
    scalars = pl.BlockSpec(memory_space=pltpu.SMEM)
    waves_out, image = pl.pallas_call(
        functools.partial(kernel, axes),
        out_shape=(pltpu.VMEM((fb * 4, SUB * strip, LANE), f32), pltpu.VMEM((plane_count, SUB * strip, LANE), f32)),
        in_specs=[pl.BlockSpec(memory_space=pltpu.HBM)] * 3 + [scalars] * 3,
        out_specs=(pl.BlockSpec(memory_space=pltpu.VMEM),) * 2,
        scratch_shapes=[
            pltpu.VMEM((fb * 4, SUB * strip, LANE), f32),
            pltpu.VMEM((fb * 4, SUB * strip, LANE), f32),
            pltpu.VMEM((plane_count, SUB * strip, LANE), f32),
            pltpu.VMEM((fb, width, 4) + TILE, f32),
            pltpu.VMEM((fb, width, 4) + TILE, f32),
            pltpu.VMEM((width, plane_count) + TILE, f32),
            pltpu.VMEM((plane_count, width, 4) + TILE, f32),
            pltpu.VMEM((fb, strip, 4) + TILE, f32),
            pltpu.VMEM((fb,) + TILE, f32),
            pltpu.VMEM((fb,) + TILE, f32),
            pltpu.VMEM((plane_count, strip) + TILE, f32),
            dma((3, fb, SUB)),
            dma((per_halo,)),
            dma((per_halo,)),
            dma((2, fb, per_halo)),
            dma((2, fb, per_halo)),
            dma((fb,)),
            dma((fb,)),
            dma((2,)),
        ],
        compiler_params=pltpu.CompilerParams(collective_id=0, has_side_effects=True, vmem_limit_bytes=32 << 20),
        name="migrate",
    )(*[pltpu.with_memory_space_constraint(x, pltpu.HBM) for x in (waves_in, surface_waves, slowness)], section_planes, block_freqs, surface_freqs)

    def rows_first(x, shape):
        return x.reshape(-1, SUB, strip, LANE).swapaxes(1, 2).reshape(shape)

    return rows_first(waves_out, waves_in.shape), rows_first(image, slowness.shape)


def solution(mesh):
    return jax.shard_map(
        local,
        mesh=mesh,
        in_specs=(
            P("depth", None, None, "lat", None),
            P(None, None, "lat", None),
            P("depth", None, "lat", None),
            P("depth"),
            P("depth", None),
            P(),
        ),
        out_specs=(P("depth", None, None, "lat", None), P("depth", None, "lat", None)),
        check_vma=False,
    )
```

```python
import functools
import math

import jax
import jax.numpy as jnp
from jax import lax
from jax.experimental import pallas as pl
from jax.experimental.pallas import tpu as pltpu
from jax.sharding import PartitionSpec as P

DEPTH_STEP = 0.02
SMOOTHING = 0.4
BASE_HERTZ = 8.0
HERTZ_STEP = 0.5
DIFFRACTION_TOP = 0.2
MIDDLE_SLOWNESS = 0.445
SIN = (0.9999999998446159, -0.16666666052254658, 0.008333294444188614, -0.0001983264692424553, 2.6775178137139403e-06)
COS = (0.9999999982977188, -0.4999999326780431, 0.04166624044803908, -0.0013879434435051892, 2.394331932466174e-05)
SUB, LANE = 8, 128
TILE = (SUB, LANE)


def horner(coefficients, t):
    value = coefficients[-1] * t + coefficients[-2]
    for c in coefficients[-3::-1]:
        value = value * t + c
    return value


def sin_cos(x):
    t = x * x
    return x * horner(SIN, t), horner(COS, t)


def constants_of(omega):
    beta = DIFFRACTION_TOP * (2.0 * math.pi * BASE_HERTZ) / omega
    rate = omega * DEPTH_STEP
    half_sin, half_cos = sin_cos(rate * (0.5 * MIDDLE_SLOWNESS))
    centre_sin, centre_cos = 2.0 * half_sin * half_cos, 1.0 - 2.0 * half_sin * half_sin
    norm = SMOOTHING * SMOOTHING + beta * beta
    g_re, g_im = SMOOTHING / norm - 2.0, -beta / norm
    a_re, a_im = SMOOTHING * SMOOTHING - beta * beta, 2.0 * SMOOTHING * beta
    k_re = a_re * centre_cos - a_im * centre_sin
    k_im = a_re * centre_sin + a_im * centre_cos
    return rate, g_re, g_im, k_re, k_im


def kernel(
    axes, waves, surface, slowness, planes_ref, freqs, surface_freqs, nat_out, nat_image,
    nat, nat_surface, nat_slow, window, window2, slow, states, outgoing, omegas, omegas2, image,
    in_sem, slow_send, slow_recv, halo_send, halo_recv, depth_send, depth_recv, omega_sem,
):
    sections, strips = axes
    s, l = lax.axis_index("depth"), lax.axis_index("lat")
    fb, plane_count = waves.shape[1], slowness.shape[1]
    halo = plane_count
    strip = waves.shape[3]
    folded = strips == 2
    top = 0 if folded else halo
    width = top + strip + halo
    following, previous = {"depth": lax.rem(s + 1, sections)}, {"depth": lax.rem(s + sections - 1, sections)}
    has_next, has_previous = s < sections - 1, s > 0

    if folded:
        other = {"lat": 1 - l}
        sides = [(None, None, other, [(strip - 1 - i, strip + i, 1) for i in range(halo)])]
    else:
        down, up = {"lat": lax.rem(l + 1, strips)}, {"lat": lax.rem(l + strips - 1, strips)}
        sides = [
            (l < strips - 1, l > 0, down, [(top + strip - halo, 0, halo)]),
            (l > 0, l < strips - 1, up, [(top, top + strip, halo)]),
        ]

    def run_if(condition, body):
        if condition is None:
            body()
        else:
            pl.when(condition)(body)

    def halo_copies(buffer, send, recv, partner, copies, first, trimmed):
        def view(row, rows, i):
            return buffer.at[pl.ds(row, rows), pl.ds(0, plane_count - i)] if trimmed and folded else buffer.at[pl.ds(row, rows)]

        return [
            pltpu.make_async_remote_copy(
                src_ref=view(row, rows, i), dst_ref=view(place, rows, i),
                send_sem=send.at[first + i], recv_sem=recv.at[first + i],
                device_id=partner, device_id_type=pl.DeviceIdType.MESH,
            )
            for i, (row, place, rows) in enumerate(copies)
        ]

    def halos(buffer, send, recv, action, trimmed=False):
        first = 0
        for can_send, can_receive, partner, copies in sides:
            descriptors = halo_copies(buffer, send, recv, partner, copies, first, trimmed)
            first += len(copies)

            def act(descriptors=descriptors):
                for copy in descriptors:
                    getattr(copy, action)()

            run_if(can_receive if action == "wait_recv" else can_send, act)

    def place_of(i):
        return i + l * (strip - 1 - 2 * i) if folded else i

    def natural(source, target, send):
        return [
            pltpu.make_async_copy(source.at[:, :, pl.ds(t * LANE, LANE)], target.at[:, pl.ds(t * strip, strip), :], send.at[t])
            for t in range(SUB)
        ]

    def waves_copies(f):
        return natural(waves.at[0, f], nat.at[pl.ds(f * 4, 4)], in_sem.at[0, f])

    def surface_copies(f):
        return natural(surface.at[f], nat_surface.at[pl.ds(f * 4, 4)], in_sem.at[1, f])

    slow_copies = natural(slowness.at[0], nat_slow, in_sem.at[2, 0])
    for copy in slow_copies:
        copy.start()
    for f in range(fb):
        for copy in waves_copies(f):
            copy.start()

    @pl.when(s == 0)
    def _():
        for f in range(fb):
            for copy in surface_copies(f):
                copy.start()

    barrier = pltpu.get_barrier_semaphore()

    def greet(partner):
        pl.semaphore_signal(barrier, inc=1, device_id=partner, device_id_type=pl.DeviceIdType.MESH)

    for can_send, _, partner, _ in sides:
        run_if(can_send, functools.partial(greet, partner))
    run_if(has_next, functools.partial(greet, following))
    run_if(has_previous, functools.partial(greet, previous))

    def omega_tile(k):
        return jnp.full(TILE, 2.0 * math.pi * (BASE_HERTZ + HERTZ_STEP * k.astype(jnp.float32)), jnp.float32)

    for f in range(fb):
        omegas[f] = omega_tile(freqs[0, f])
    image[...] = jnp.zeros_like(image)
    if not folded:
        for f in range(fb):
            for buffer in (window, window2):
                buffer[f, :top] = jnp.zeros_like(buffer[f, :top])
                buffer[f, top + strip :] = jnp.zeros_like(buffer[f, top + strip :])
        slow[:top] = jnp.zeros_like(slow[:top])
        slow[top + strip :] = jnp.zeros_like(slow[top + strip :])
    for copy in slow_copies:
        copy.wait()
    for p in range(plane_count):
        for i in range(strip):
            slow[top + i, p] = nat_slow[p, pl.ds(place_of(i), SUB, stride=strip), :]

    peers = jnp.where(has_next, 1, 0) + jnp.where(has_previous, 1, 0)
    for can_send, _, _, _ in sides:
        peers = peers + (1 if can_send is None else jnp.where(can_send, 1, 0))
    pl.semaphore_wait(barrier, peers)

    omega_copy = pltpu.make_async_remote_copy(
        src_ref=omegas, dst_ref=omegas2, send_sem=omega_sem.at[0], recv_sem=omega_sem.at[1],
        device_id=following, device_id_type=pl.DeviceIdType.MESH,
    )
    halos(slow, slow_send, slow_recv, "start", True)
    run_if(has_next, omega_copy.start)

    def relayout(source, target, f):
        for i in range(strip):
            for c in range(4):
                target[f, top + i, c] = source[f * 4 + c, pl.ds(place_of(i), SUB, stride=strip), :]

    @pl.loop(0, fb)
    def _(f):
        for copy in waves_copies(f):
            copy.wait()
        relayout(nat, window, f)
        halos(window.at[f], halo_send.at[0, f], halo_recv.at[0, f], "start")

    row_of = lax.broadcasted_iota(jnp.int32, TILE, 0)
    lane_of = lax.broadcasted_iota(jnp.int32, TILE, 1)
    first_lane, last_lane = lane_of == 0, lane_of == LANE - 1
    first_row, last_row = row_of == 0, row_of == SUB - 1

    def beside(u):
        left = pltpu.roll(u, 1, 1)
        right = pltpu.roll(u, LANE - 1, 1)
        before = jnp.where(first_row, 0.0, pltpu.roll(left, 1, 0))
        after = jnp.where(last_row, 0.0, pltpu.roll(right, SUB - 1, 0))
        return jnp.where(first_lane, before, left) + jnp.where(last_lane, after, right)

    def section(load, omega):
        rate, g_re, g_im, k_re, k_im = constants_of(omega)

        def spread(u, total):
            s_re, s_im, r_re, r_im = u
            return (
                g_re * s_re - g_im * s_im + total[0],
                g_re * s_im + g_im * s_re + total[1],
                g_re * r_re + g_im * r_im + total[2],
                g_re * r_im - g_im * r_re + total[3],
            )

        def rotated(p, j):
            sin, cos = sin_cos((slow[j, p] - MIDDLE_SLOWNESS) * rate)
            e_re, e_im = k_re * cos - k_im * sin, k_re * sin + k_im * cos
            s_re, s_im, r_re, r_im = [load(j, c) if p == 0 else states[p - 1, j, c] for c in range(4)]
            return (
                s_re * e_re - s_im * e_im,
                s_re * e_im + s_im * e_re,
                r_re * e_re + r_im * e_im,
                r_im * e_re - r_re * e_im,
            )

        for p in range(plane_count):
            low, high = (0 if folded else p + 1), width - 1 - p
            behind = None if folded else rotated(p, low - 1)
            here = rotated(p, low)
            for j in range(low, high):
                ahead = rotated(p, j + 1)
                total = ahead if behind is None else [x + y for x, y in zip(behind, ahead)]
                u = spread(here, total)
                if j < top:
                    u = [jnp.where(l > 0, x, 0.0) for x in u]
                elif j >= top + strip and not folded:
                    u = [jnp.where(l < strips - 1, x, 0.0) for x in u]
                u = spread(u, [beside(x) for x in u])
                for c in range(4):
                    states[p, j, c] = u[c]
                if top <= j < top + strip:
                    image[p, j - top] += u[0] * u[2] + u[1] * u[3]
                behind, here = here, ahead

    last_plane = jnp.clip(planes_ref[0] - 1, 0, plane_count - 1)

    pieces = [(strip - halo, halo), (0, strip - halo)] if folded and halo < strip else [(0, strip)]

    def depth_copies(f):
        return [
            pltpu.make_async_remote_copy(
                src_ref=outgoing.at[f, pl.ds(row, rows)], dst_ref=window2.at[f, pl.ds(top + row, rows)],
                send_sem=depth_send.at[f, k], recv_sem=depth_recv.at[f, k],
                device_id=following, device_id_type=pl.DeviceIdType.MESH,
            )
            for k, (row, rows) in enumerate(pieces)
        ]

    def arrive(f):
        @pl.when(has_previous)
        def _():
            depth_copies(f)[0].wait_recv()

        @pl.when(s == 0)
        def _():
            for copy in surface_copies(f):
                copy.wait()
            relayout(nat_surface, window2, f)

        halos(window2.at[f], halo_send.at[1, f], halo_recv.at[1, f], "start")

    lag = min(2, fb)

    halos(slow, slow_send, slow_recv, "wait_recv", True)

    @pl.loop(0, fb)
    def _(f):
        halos(window.at[f], halo_send.at[0, f], halo_recv.at[0, f], "wait_recv")
        section(lambda j, c: window[f, j, c], omegas[f])
        for i in range(strip):
            for c in range(4):
                outgoing[f, i, c] = states[last_plane, top + i, c]

        @pl.when(has_next)
        def _():
            for copy in depth_copies(f):
                copy.start()

        @pl.when(f >= lag)
        def _():
            arrive(f - lag)

    @pl.when(has_previous)
    def _():
        omega_copy.wait_recv()

    @pl.when(s == 0)
    def _():
        for f in range(fb):
            omegas2[f] = omega_tile(surface_freqs[f])

    for f in range(fb - lag, lag):
        arrive(f)

    @pl.loop(0, fb)
    def _(f):
        @pl.when(f < fb - lag)
        def _():
            arrive(f + lag)

        @pl.when(has_previous)
        def _():
            for copy in depth_copies(f)[1:]:
                copy.wait_recv()

        halos(window2.at[f], halo_send.at[1, f], halo_recv.at[1, f], "wait_recv")
        section(lambda j, c: window2[f, j, c], omegas2[f])
        for i in range(strip):
            for c in range(4):
                nat_out[f * 4 + c, pl.ds(place_of(i), SUB, stride=strip), :] = states[last_plane, top + i, c]

    for p in range(plane_count):
        weight = jnp.where(p <= last_plane, 1.0 / fb, 0.0)
        for i in range(strip):
            nat_image[p, pl.ds(place_of(i), SUB, stride=strip), :] = image[p, i] * weight
    halos(slow, slow_send, slow_recv, "wait_send", True)

    @pl.when(has_next)
    def _():
        omega_copy.wait_send()
        for f in range(fb):
            for copy in depth_copies(f):
                copy.wait_send()

    for f in range(fb):
        halos(window.at[f], halo_send.at[0, f], halo_recv.at[0, f], "wait_send")
        halos(window2.at[f], halo_send.at[1, f], halo_recv.at[1, f], "wait_send")


def local(waves_in, surface_waves, slowness, section_planes, block_freqs, surface_freqs):
    axes = (lax.axis_size("depth"), lax.axis_size("lat"))
    _, fb, _, strip, columns = waves_in.shape
    plane_count = slowness.shape[1]
    if columns != SUB * LANE or strip != SUB:
        raise ValueError("unsupported strip")
    folded = axes[1] == 2
    width = (0 if folded else plane_count) + strip + plane_count
    per_halo = plane_count if folded else 2
    f32 = jnp.float32
    dma = pltpu.SemaphoreType.DMA
    anywhere = pl.BlockSpec(memory_space=pl.ANY)
    scalars = pl.BlockSpec(memory_space=pltpu.SMEM)
    waves_out, image = pl.pallas_call(
        functools.partial(kernel, axes),
        out_shape=(pltpu.VMEM((fb * 4, SUB * strip, LANE), f32), pltpu.VMEM((plane_count, SUB * strip, LANE), f32)),
        in_specs=[pl.BlockSpec(memory_space=pltpu.HBM)] * 3 + [scalars] * 3,
        out_specs=(pl.BlockSpec(memory_space=pltpu.VMEM),) * 2,
        scratch_shapes=[
            pltpu.VMEM((fb * 4, SUB * strip, LANE), f32),
            pltpu.VMEM((fb * 4, SUB * strip, LANE), f32),
            pltpu.VMEM((plane_count, SUB * strip, LANE), f32),
            pltpu.VMEM((fb, width, 4) + TILE, f32),
            pltpu.VMEM((fb, width, 4) + TILE, f32),
            pltpu.VMEM((width, plane_count) + TILE, f32),
            pltpu.VMEM((plane_count, width, 4) + TILE, f32),
            pltpu.VMEM((fb, strip, 4) + TILE, f32),
            pltpu.VMEM((fb,) + TILE, f32),
            pltpu.VMEM((fb,) + TILE, f32),
            pltpu.VMEM((plane_count, strip) + TILE, f32),
            dma((3, fb, SUB)),
            dma((per_halo,)),
            dma((per_halo,)),
            dma((2, fb, per_halo)),
            dma((2, fb, per_halo)),
            dma((fb, 2)),
            dma((fb, 2)),
            dma((2,)),
        ],
        compiler_params=pltpu.CompilerParams(collective_id=0, has_side_effects=True, vmem_limit_bytes=32 << 20),
        name="migrate",
    )(*[pltpu.with_memory_space_constraint(x, pltpu.HBM) for x in (waves_in, surface_waves, slowness)], section_planes, block_freqs, surface_freqs)

    def rows_first(x, shape):
        return x.reshape(-1, SUB, strip, LANE).swapaxes(1, 2).reshape(shape)

    return rows_first(waves_out, waves_in.shape), rows_first(image, slowness.shape)


def solution(mesh):
    return jax.shard_map(
        local,
        mesh=mesh,
        in_specs=(
            P("depth", None, None, "lat", None),
            P(None, None, "lat", None),
            P("depth", None, "lat", None),
            P("depth"),
            P("depth", None),
            P(),
        ),
        out_specs=(P("depth", None, None, "lat", None), P("depth", None, "lat", None)),
        check_vma=False,
    )
```
